32 devices in a mesh: row: 4 (over z), col: 8 (over y, x, core).
Axes of the slice: x: 2, y: 2, z: 4, core: 2. Of those that a mesh axis runs over, the one named last changes fastest.
Arguments:
- fem_basis: float32 [2, 16, 2, 65536], P(None, None, None, ('row', 'col')), may hold values from -8 to 8
- bem_basis: float32 [2, 16, 2, 16384], P(None, None, None, ('row', 'col')), may hold values from -8 to 8
- fem_diagonal: float32 [65536], P(('row', 'col')), may hold values from 1 to 4
- fem_values: float32 [16, 65536], P(None, ('row', 'col')), may hold values from -1.5 to 1.5
- fem_columns: int32 [16, 65536], P(None, ('row', 'col')), may hold values from 0 to 2559
- halo_rows: int32 [4, 4096], P(None, ('row', 'col')), may hold values from 0 to 2047
- bem_matrix: bfloat16 [2, 16384, 16384], P(None, 'row', 'col'), may hold values from -0.03125 to 0.03125
- trace_rows: int32 [32768], P(('row', 'col')), may hold values from -1 to 2047, as said below
- bem_slot: int32 [16384], P(('row', 'col')), may hold values from 0 to 1023, as said below
Outputs:
- next_fem: float32 [16, 2, 65536], P(None, None, ('row', 'col'))
- next_bem: float32 [16, 2, 16384], P(None, None, ('row', 'col'))
- hessenberg: float32 [2, 16, 16], replicated
- r_factor: float32 [16, 16], replicated
The draws below stay inside these ranges and needn't reach their ends.
Inputs may be any that keep to these rules, and one draw needn't show every extreme that they name: `trace_rows`: each device's entries form one block of 32 slots per BEM owner, owners in row+col order; a block is all -1 (unused) or holds local FEM rows, the rows of one device being distinct; every owner is fed by exactly 16 full blocks. `bem_slot`: value = source device along row+col times 32 plus slot; within one owner the values are distinct and are exactly the full slots that trace_rows sends to that owner.
All inputs are finite; a program needn't handle non-finite values.
Results may differ from the reference program's by a relative error of at most 0.0014.
Values may be sent and summed in bfloat16 or wider, within the bound.
No kernel may reach another device: no remote copies, remote signals or barrier semaphores. Data moves between devices by JAX's collectives and lax.ppermute only.
A program may use at most 128 MiB of HBM per device.

```python
import math
import jax
import jax.numpy as jnp
from jax import lax

NRHS = 16
BLOCKS = 2
NZ = 16
ROWS_DEV = 2048
NBEM = 16384
HALO = 128
PIECE = 512
PICK = 16
TSLOT = 32
SLOTS = 1024
NFEM = 65536
N_ROW = 4
N_COL = 8
DEVICES = 32


def basis_draw(key, length):
    extent = (BLOCKS, NRHS, 2, length)
    common = jax.random.normal(jax.random.fold_in(key, 11), (1, NRHS, 2, length), jnp.float32)
    private = jax.random.normal(jax.random.fold_in(key, 12), extent, jnp.float32)
    return jnp.clip((private + 0.7 * common) / 1.22, -8.0, 8.0)


def draw_fem_basis(key, part):
    return basis_draw(key, NFEM)


def draw_bem_basis(key, part):
    return basis_draw(jax.random.fold_in(key, 5), NBEM)


def trace_plan(key):
    base = jax.random.fold_in(key, 29)
    levels = jax.random.randint(jax.random.fold_in(base, 1), (DEVICES,), 0, 4) * 96
    jitter = jax.random.randint(jax.random.fold_in(base, 2), (DEVICES, DEVICES), 0, 256)
    sources = jnp.arange(DEVICES, dtype=jnp.int32)
    scores = (levels[None, :] + jitter) * DEVICES + sources[None, :]
    picked = lax.top_k(scores, PICK)[1].astype(jnp.int32)
    order_keys = jax.random.randint(jax.random.fold_in(base, 3), (DEVICES, PIECE), 0, 1 << 20) * PIECE + jnp.arange(PIECE, dtype=jnp.int32)[None, :]
    placing = jnp.argsort(order_keys, axis=1).astype(jnp.int32)
    inverse = jnp.argsort(placing, axis=1).astype(jnp.int32)
    slot_of_position = (picked[:, :, None] * TSLOT + jnp.arange(TSLOT, dtype=jnp.int32)[None, None, :]).reshape(DEVICES, PIECE)
    slot_table = jnp.take_along_axis(slot_of_position, inverse, axis=1)
    row_keys = jax.random.randint(jax.random.fold_in(base, 4), (DEVICES, ROWS_DEV), 0, 1 << 12) * ROWS_DEV + jnp.arange(ROWS_DEV, dtype=jnp.int32)[None, :]
    rows_order = jnp.argsort(row_keys, axis=1)[:, :SLOTS].astype(jnp.int32)
    chosen = jnp.any(picked[:, :, None] == sources[None, None, :], axis=1)
    chosen_rows = jnp.repeat(chosen.T, TSLOT, axis=1)
    rows_table = jnp.where(chosen_rows, rows_order, -1).astype(jnp.int32)
    return (rows_table.reshape(-1), slot_table.reshape(-1))


def draw_trace_rows(key, part):
    return trace_plan(key)[0]


def draw_bem_slot(key, part):
    return trace_plan(key)[1]


def with_ends(array, key, smallest, high):
    place = [jax.random.randint(jax.random.fold_in(key, axis), (), 0, length) for axis, length in enumerate(array.shape)]
    main_axis = array.shape.index(max(array.shape))
    beside = place[:main_axis] + [(place[main_axis] + 1) % array.shape[main_axis]] + place[main_axis + 1:]
    return array.at[tuple(place)].set(smallest).at[tuple(beside)].set(high)


def level_of(rng, shape, split, least, high):
    gain = 1.0
    for dim, shards_of in split:
        steps = jax.random.uniform(jax.random.fold_in(jax.random.fold_in(rng, 6), dim), (shards_of,), jnp.float32, least / len(split), high / len(split))
        gain = gain * jnp.repeat(jnp.exp(steps), shape[dim] // shards_of).reshape((-1,) + (1,) * (len(shape) - 1 - dim))
    return gain


def bell_draw(own_key, shape, spread, bound, cuts=(), kind=jnp.bfloat16):
    level = level_of(own_key, shape, cuts, -0.22, 0.18) if cuts else 1.0
    drawn = jax.random.normal(own_key, shape, jnp.float32) * spread * level
    return jnp.minimum(jnp.maximum(drawn, -bound), bound).astype(kind)


def setup_inputs(seed: int = 0) -> dict:
    arg_keys = jax.random.split(jax.random.key(seed), 10)
    return {
        "fem_basis": draw_fem_basis(jax.random.fold_in(arg_keys[9], 71), 0),
        "bem_basis": draw_bem_basis(jax.random.fold_in(arg_keys[9], 71), 0),
        "fem_diagonal": jnp.clip(jnp.exp(math.log(4.0) - 1.3862944 * jax.random.uniform(arg_keys[2], (NFEM,), jnp.float32) ** level_of(arg_keys[2], (NFEM,), ((0, 32),), -0.2, 0.2)), 1.0, 4.0),
        "fem_values": bell_draw(arg_keys[3], (NZ, NFEM), NZ ** -0.5, 1.5, ((1, 32),), jnp.float32),
        "fem_columns": with_ends(jax.random.randint(arg_keys[4], (NZ, NFEM), 0, ROWS_DEV + 4 * HALO), jax.random.fold_in(arg_keys[4], 1), 0, (ROWS_DEV + 4 * HALO) - 1).astype(jnp.int32),
        "halo_rows": with_ends(jax.random.randint(arg_keys[5], (4, DEVICES * HALO), 0, ROWS_DEV), jax.random.fold_in(arg_keys[5], 1), 0, ROWS_DEV - 1).astype(jnp.int32),
        "bem_matrix": bell_draw(arg_keys[6], (2, NBEM, NBEM), (2 * NBEM) ** -0.5, 0.03125, ((1, 4), (2, 8))),
        "trace_rows": draw_trace_rows(jax.random.fold_in(arg_keys[9], 71), 0),
        "bem_slot": draw_bem_slot(jax.random.fold_in(arg_keys[9], 71), 0),
    }


HIGHEST = lax.Precision.HIGHEST

def dotted(lefts, rights):
    return lax.dot_general(lefts.reshape(lefts.shape[0], -1).astype(jnp.float32), rights.reshape(rights.shape[0], -1).astype(jnp.float32), (((1,), (1,)), ((), ())), precision=HIGHEST, preferred_element_type=jnp.float32)

def combine(coeffs, basis):
    flat_basis = basis.reshape(basis.shape[0], -1)
    merged = lax.dot_general(coeffs.astype(jnp.float32), flat_basis.astype(jnp.float32), (((0,), (0,)), ((), ())), precision=HIGHEST, preferred_element_type=jnp.float32)
    return merged.reshape((coeffs.shape[1],) + basis.shape[1:])

def shifted(blocks, axis_pos, forward):
    widths = [(0, 0)] * blocks.ndim
    widths[axis_pos] = (1, 0) if forward else (0, 1)
    padded = jnp.pad(blocks, widths)
    if forward:
        return lax.slice_in_dim(padded, 0, blocks.shape[axis_pos], axis=axis_pos)
    return lax.slice_in_dim(padded, 1, blocks.shape[axis_pos] + 1, axis=axis_pos)

def fem_apply(vectors, fem_diagonal, fem_values, fem_columns, halo_rows):
    lists = halo_rows.reshape(4, N_ROW, N_COL, HALO)
    values = fem_values.reshape(NZ, N_ROW, N_COL, ROWS_DEV)
    columns = fem_columns.reshape(NZ, N_ROW, N_COL, ROWS_DEV)
    diagonal = fem_diagonal.reshape(N_ROW, N_COL, ROWS_DEV)

    def single(one_vector):
        outbound = [jnp.take_along_axis(one_vector, lists[direction], axis=2) for direction in range(4)]
        extended = jnp.concatenate([one_vector, shifted(outbound[0], 1, True), shifted(outbound[1], 1, False), shifted(outbound[2], 0, True), shifted(outbound[3], 0, False)], axis=2)

        def accumulate(position, accrued):
            return accrued + values[position] * jnp.take_along_axis(extended, columns[position], axis=2)
        return lax.fori_loop(0, NZ, accumulate, diagonal * one_vector)
    stacked = vectors.reshape(NRHS * 2, N_ROW, N_COL, ROWS_DEV)
    return lax.map(single, stacked).reshape(NRHS, 2, NFEM)

def bem_apply(vectors, bem_matrix):
    piece_len = NBEM // (N_ROW * N_COL)
    rounded = vectors.astype(jnp.bfloat16).reshape(NRHS * 2, N_ROW, N_COL, piece_len)
    stored = jnp.transpose(rounded, (0, 2, 1, 3)).reshape(NRHS * 2, NBEM)
    real_mat = lax.dot_general(stored.astype(jnp.float32), bem_matrix[0].astype(jnp.float32), (((1,), (1,)), ((), ())), preferred_element_type=jnp.float32).reshape(NRHS, 2, NBEM)
    imag_mat = lax.dot_general(stored.astype(jnp.float32), bem_matrix[1].astype(jnp.float32), (((1,), (1,)), ((), ())), preferred_element_type=jnp.float32).reshape(NRHS, 2, NBEM)
    return jnp.stack([real_mat[:, 0] - imag_mat[:, 1], imag_mat[:, 0] + real_mat[:, 1]], axis=1)

def trace_index(trace_rows, bem_slot):
    piece_len = NBEM // (N_ROW * N_COL)
    owners = jnp.arange(NBEM, dtype=jnp.int32) // piece_len
    sources = bem_slot // TSLOT
    within = bem_slot % TSLOT
    rows_at = trace_rows[sources * SLOTS + owners * TSLOT + within]
    return (sources * ROWS_DEV + rows_at).astype(jnp.int32)

def reference(fem_basis, bem_basis, fem_diagonal, fem_values, fem_columns, halo_rows, bem_matrix, trace_rows, bem_slot):
    fem_last = fem_basis[BLOCKS - 1]
    bem_last = bem_basis[BLOCKS - 1]
    positions = trace_index(trace_rows, bem_slot)
    fem_image = fem_apply(fem_last, fem_diagonal, fem_values, fem_columns, halo_rows)
    bem_image = bem_apply(bem_last, bem_matrix) + fem_last[:, :, positions]
    fem_image = fem_image.at[:, :, positions].add(bem_last)
    count = 2.0 * (NFEM + NBEM)
    fem_flat = fem_basis.reshape(BLOCKS * NRHS, 2, NFEM)
    bem_flat = bem_basis.reshape(BLOCKS * NRHS, 2, NBEM)
    coeffs_one = (dotted(fem_flat, fem_image) + dotted(bem_flat, bem_image)) / count
    fem_once = fem_image - combine(coeffs_one, fem_flat)
    bem_once = bem_image - combine(coeffs_one, bem_flat)
    coeffs_two = (dotted(fem_flat, fem_once) + dotted(bem_flat, bem_once)) / count
    fem_twice = fem_once - combine(coeffs_two, fem_flat)
    bem_twice = bem_once - combine(coeffs_two, bem_flat)
    gram_matrix = (dotted(fem_twice, fem_twice) + dotted(bem_twice, bem_twice)) / count
    lower_factor = jnp.linalg.cholesky(gram_matrix)
    inverse_lower = jax.scipy.linalg.solve_triangular(lower_factor, jnp.eye(NRHS, dtype=jnp.float32), lower=True)
    next_fem = combine(inverse_lower.T, fem_twice)
    next_bem = combine(inverse_lower.T, bem_twice)
    hessenberg = (coeffs_one + coeffs_two).reshape(BLOCKS, NRHS, NRHS)
    return (next_fem, next_bem, hessenberg, lower_factor.T)
```

```python
import functools

import jax
import jax.numpy as jnp
from jax import lax
from jax.experimental import pallas as pl
from jax.experimental.pallas import tpu as pltpu
from jax.sharding import PartitionSpec as P

F32 = jnp.float32
BF16 = jnp.bfloat16
I32 = jnp.int32
HIGHEST = lax.Precision.HIGHEST
LANES = 128
SUB = 8
NT = (((1,), (1,)), ((), ()))
NN = (((1,), (0,)), ((), ()))
ANY = pl.BlockSpec(memory_space=pl.ANY)


def rows8(block, k):
    return jnp.broadcast_to(block[k : k + 1], (SUB, LANES))


def lookup(load, index, chunks, groups, first=0):
    lane = index & (LANES - 1)
    chunk = index >> 7
    picked = [jnp.zeros((SUB, LANES), F32) for _ in range(groups)]
    for c in range(first, chunks):
        here = chunk == c
        for g in range(groups):
            taken = jnp.take_along_axis(load(g, c), lane, axis=1)
            picked[g] = jnp.where(here, taken, picked[g])
    return picked


def chunk_of(ref, base=0):
    def load(g, c):
        return ref[base + SUB * g : base + SUB * (g + 1), LANES * c : LANES * (c + 1)]

    return load


def across(index_row):
    return jnp.transpose(jnp.broadcast_to(index_row, (LANES, LANES)))


def inverse(columns, count, wanted):
    best = jnp.full((SUB, LANES), -1, I32)
    sub = lax.broadcasted_iota(I32, (SUB, LANES), 0)
    for r in range(count // SUB):
        best = jnp.where(columns(r) == wanted, sub + SUB * r, best)
    top = jnp.max(best.astype(F32), axis=0, keepdims=True).astype(I32)
    return jnp.broadcast_to(top, (SUB, LANES))


def lane_ids():
    return lax.broadcasted_iota(I32, (SUB, LANES), 1)


def start_all(copies):
    for copy in copies:
        copy.start()
    return copies


def wait_all(copies):
    for copy in copies:
        copy.wait()


def send_kernel(sizes, fem_hbm, bem_hbm, halo_ref, trace_ref, slot_ref, u_ref, out_ref, mail_ref, phi_ref, bem_ref, col_ref, sem):
    blocks, rhs, nf, nb, width, slots, fold = sizes
    groups = 2 * rhs // SUB
    copies = start_all(
        [pltpu.make_async_copy(bem_hbm.at[blocks - 1, :, p, :], bem_ref.at[pl.ds(rhs * p, rhs), :], sem.at[p]) for p in range(2)]
        + [pltpu.make_async_copy(fem_hbm.at[blocks - 1, :, p, :], u_ref.at[pl.ds(rhs * p, rhs), :], sem.at[2 + p]) for p in range(2)]
    )
    for c in range(nb // LANES):
        col_ref[LANES * c : LANES * (c + 1), :] = across(slot_ref[c : c + 1, :])
    owners = []
    for t in range(slots // LANES):
        owners.append(
            inverse(lambda r: col_ref[SUB * r : SUB * (r + 1), :], nb, lane_ids() + LANES * t)
        )
    wait_all(copies)
    phi_ref[...] = bem_ref[...].astype(BF16)
    for d in range(4):
        for t in range(width // LANES):
            index = rows8(halo_ref[:, LANES * t : LANES * (t + 1)], d)
            for g, got in enumerate(lookup(chunk_of(u_ref), index, nf // LANES, groups)):
                out_ref[d, SUB * g : SUB * (g + 1), LANES * t : LANES * (t + 1)] = got
    for t in range(slots // LANES):
        index = rows8(trace_ref[...], t)
        ask = lookup(chunk_of(u_ref), jnp.where(index >= 0, index, -LANES), nf // LANES, groups)
        give = lookup(chunk_of(bem_ref), owners[t], nb // LANES, groups)
        if fold:
            lane_block = lane_ids() // (LANES // fold)
            for e in range(fold):
                for h, parts in enumerate((ask, give)):
                    for b in range(groups // fold):
                        sheet = None
                        for q in range(fold):
                            moved = parts[b * fold + q]
                            shift = ((q - e) * (LANES // fold)) % LANES
                            moved = pltpu.roll(moved, shift, 1) if shift else moved
                            sheet = moved if sheet is None else jnp.where(lane_block == q, moved, sheet)
                        at = SUB * (h * (groups // fold) + b)
                        mail_ref[t * fold + e, at : at + SUB, :] = sheet
        else:
            for g in range(groups):
                mail_ref[SUB * g : SUB * (g + 1), LANES * t : LANES * (t + 1)] = ask[g]
                mail_ref[2 * rhs + SUB * g : 2 * rhs + SUB * (g + 1), LANES * t : LANES * (t + 1)] = give[g]


def fem_tile(t, sizes, span, u_ref, halo_refs, col_ref, val_ref, start):
    rhs, nf, width, nz = sizes
    groups = 2 * rhs // SUB
    first, last = span
    inner = nf // LANES
    per = width // LANES
    at = pl.ds(pl.multiple_of(t * LANES, LANES), LANES)

    def load(g, c):
        if c < inner:
            return u_ref[SUB * g : SUB * (g + 1), LANES * c : LANES * (c + 1)]
        d, w = divmod(c - inner, per)
        return halo_refs[d][SUB * g : SUB * (g + 1), LANES * w : LANES * (w + 1)]

    sums = start(at)
    for kk in range(nz // SUB):
        cols = col_ref[SUB * kk : SUB * (kk + 1), at]
        vals = val_ref[SUB * kk : SUB * (kk + 1), at]
        for k in range(SUB):
            got = lookup(load, rows8(cols, k), last, groups, first)
            weight = rows8(vals, k)
            sums = [s + weight * x for s, x in zip(sums, got)]
    return at, sums


def own_kernel(sizes, tiles, u_ref, col_ref, val_ref, diag_ref, o_ref):
    rhs, nf, _, _ = sizes

    def start(at):
        scale = diag_ref[pl.ds(0, 1), at]
        return [u_ref[SUB * g : SUB * (g + 1), at] * scale for g in range(2 * rhs // SUB)]

    def step(t, carry):
        at, sums = fem_tile(t, sizes, (0, nf // LANES), u_ref, None, col_ref, val_ref, start)
        for g, s in enumerate(sums):
            o_ref[SUB * g : SUB * (g + 1), at] = s
        return carry

    lax.fori_loop(0, tiles, step, 0)


def bem_kernel(sizes, tiles, each, phi_ref, m_ref, u_ref, h0, h1, h2, h3, col_ref, val_ref, diag_ref, part_ref, o_ref, f_ref):
    rhs, nf, width, nz = sizes
    i = pl.program_id(0)
    phi = jnp.concatenate([phi_ref[r] for r in range(phi_ref.shape[0])], axis=1)
    p0 = lax.dot_general(phi, m_ref[0], NT, preferred_element_type=F32)
    p1 = lax.dot_general(phi, m_ref[1], NT, preferred_element_type=F32)
    o_ref[0, 0:rhs] = p0[0:rhs] - p1[rhs:]
    o_ref[0, rhs:] = p1[0:rhs] + p0[rhs:]
    halos = (h0, h1, h2, h3)
    inner = nf // LANES
    outer = inner + 4 * (width // LANES)

    def step(j, carry):
        t = i * each + j

        def own(at):
            return [part_ref[SUB * g : SUB * (g + 1), at] for g in range(2 * rhs // SUB)]

        def fresh(at):
            scale = diag_ref[pl.ds(0, 1), at]
            return [u_ref[SUB * g : SUB * (g + 1), at] * scale for g in range(2 * rhs // SUB)]

        @pl.when(t < tiles)
        def _():
            at, sums = fem_tile(t, sizes, (inner, outer), u_ref, halos, col_ref, val_ref, own)
            for g, s in enumerate(sums):
                f_ref[SUB * g : SUB * (g + 1), at] = s

        @pl.when(t >= tiles)
        def _():
            at, sums = fem_tile(t, sizes, (0, outer), u_ref, halos, col_ref, val_ref, fresh)
            for g, s in enumerate(sums):
                f_ref[SUB * g : SUB * (g + 1), at] = s

        return carry

    lax.fori_loop(0, each, step, 0)


def split(x):
    high = x.astype(BF16)
    return high, (x - high.astype(F32)).astype(BF16)


def products(q, w):
    rows = jnp.concatenate([q, w], axis=0)
    pad = jnp.zeros((LANES - rows.shape[0], rows.shape[1]), F32)
    high, low = split(rows)
    high_all, low_all = split(jnp.concatenate([rows, pad], axis=0))
    total = lax.dot_general(high, high_all, NT, preferred_element_type=F32)
    total += lax.dot_general(high, low_all, NT, preferred_element_type=F32)
    total += lax.dot_general(low, high_all, NT, preferred_element_type=F32)
    return total


def trace_kernel(sizes, fem_hbm, f_ref, mail_ref, trace_ref, slot_ref, w_ref, add_ref, z_ref, col_ref, got_ref, q_ref, sem):
    blocks, rhs, nf, nb, width, slots, fold = sizes
    groups = 2 * rhs // SUB
    copies = start_all(
        [
            pltpu.make_async_copy(fem_hbm.at[b, :, p, :], q_ref.at[p, pl.ds(rhs * b, rhs), :], sem.at[2 * b + p])
            for b in range(blocks)
            for p in range(2)
        ]
    )
    for c in range(slots // LANES):
        col_ref[LANES * c : LANES * (c + 1), :] = across(trace_ref[c : c + 1, :])
    if fold:
        lane_block = lane_ids() // (LANES // fold)
        for t in range(slots // LANES):
            for h in range(2):
                for g in range(groups):
                    b, q = divmod(g, fold)
                    at = SUB * (h * (groups // fold) + b)
                    sheet = None
                    for e in range(fold):
                        moved = mail_ref[t * fold + e, at : at + SUB, :]
                        shift = ((e - q) * (LANES // fold)) % LANES
                        moved = pltpu.roll(moved, shift, 1) if shift else moved
                        sheet = moved if sheet is None else jnp.where(lane_block == e, moved, sheet)
                    row = 2 * rhs * h + SUB * g
                    got_ref[row : row + SUB, LANES * t : LANES * (t + 1)] = sheet
    else:
        got_ref[...] = mail_ref[...]
    for t in range(nb // LANES):
        index = rows8(slot_ref[...], t)
        for g, got in enumerate(lookup(chunk_of(got_ref), index, slots // LANES, groups)):
            add_ref[SUB * g : SUB * (g + 1), LANES * t : LANES * (t + 1)] = got

    def step(t, carry):
        at = pl.ds(pl.multiple_of(t * LANES, LANES), LANES)
        index = inverse(lambda r: col_ref[SUB * r : SUB * (r + 1), :], slots, lane_ids() + LANES * t)
        for g, got in enumerate(lookup(chunk_of(got_ref, 2 * rhs), index, slots // LANES, groups)):
            w_ref[SUB * g : SUB * (g + 1), at] = f_ref[SUB * g : SUB * (g + 1), at] + got
        return carry

    lax.fori_loop(0, nf // LANES, step, 0)
    wait_all(copies)
    z_ref[...] = products(q_ref[0], w_ref[0:rhs]) + products(q_ref[1], w_ref[rhs:])


def sums_kernel(sizes, bem_hbm, parts_ref, add_ref, z_ref, w_ref, o_ref, q_ref, sem):
    blocks, rhs = sizes
    copies = start_all(
        [
            pltpu.make_async_copy(bem_hbm.at[b, :, p, :], q_ref.at[p, pl.ds(rhs * b, rhs), :], sem.at[2 * b + p])
            for b in range(blocks)
            for p in range(2)
        ]
    )
    total = add_ref[...]
    for d in range(parts_ref.shape[0]):
        total = total + parts_ref[d]
    w_ref[...] = total
    wait_all(copies)
    z = z_ref[...] + products(q_ref[0], total[0:rhs]) + products(q_ref[1], total[rhs:])
    basis = blocks * rhs
    lane = lax.broadcasted_iota(I32, (rhs, LANES), 1)
    packed = z[basis:]
    for b in range(blocks):
        shift = LANES - basis * (blocks - b)
        packed = packed + pltpu.roll(jnp.where(lane < basis, z[rhs * b : rhs * (b + 1)], 0.0), shift, 1)
    o_ref[...] = packed


def factor(gram, rhs):
    row = lax.broadcasted_iota(I32, (rhs, LANES), 0)
    lane = lax.broadcasted_iota(I32, (rhs, LANES), 1)
    work = jnp.where(lane == row + rhs, 1.0, gram)
    done = jnp.zeros((rhs, LANES), F32)
    for k in range(rhs):
        pivot = jnp.broadcast_to(work[k : k + 1, k : k + 1], (1, LANES))
        line = work[k : k + 1, :] / jnp.sqrt(pivot)
        scale = line[:, k : k + 1]
        column = jnp.sum(jnp.where(lane == k, work, 0.0), axis=1, keepdims=True)
        done = jnp.where(row == k, line, done)
        work = work - (column / scale) * line
    return done


def last_kernel(sizes, fem_hbm, bem_hbm, all_ref, wf_ref, wb_ref, nf_hbm, nb_hbm, h_ref, r_ref, q_ref, b_ref, of_ref, ob_ref, sem):
    blocks, rhs, count = sizes
    basis = blocks * rhs
    copies = start_all(
        [
            pltpu.make_async_copy(hbm.at[b, :, p, :], ref.at[p, pl.ds(rhs * b, rhs), :], sem.at[s, 2 * b + p])
            for s, (hbm, ref) in enumerate(((fem_hbm, q_ref), (bem_hbm, b_ref)))
            for b in range(blocks)
            for p in range(2)
        ]
    )
    total = all_ref[0]
    for d in range(1, all_ref.shape[0]):
        total = total + all_ref[d]
    total = total / count
    c1 = total[:, 0:basis]
    g = jnp.concatenate(
        [pltpu.roll(total, basis * (blocks - b), 1)[:, 0:basis] for b in range(blocks)], axis=0
    )
    lane = lax.broadcasted_iota(I32, (rhs, LANES), 1)
    own = jnp.where(lane < rhs, pltpu.roll(total, LANES - basis, 1), 0.0)

    def dot(x, y, dims):
        return lax.dot_general(x, y, dims, precision=HIGHEST, preferred_element_type=F32)

    c2 = c1 - dot(c1, g, NN)
    h = c1 + c2
    rest = 2.0 * c1 - dot(h, g, NN)
    rest_pad = jnp.concatenate([rest, jnp.zeros((LANES - rhs, basis), F32)], axis=0)
    gram = own - dot(h, rest_pad, NT)
    gram = jnp.where(lane < rhs, gram, 0.0)
    done = factor(gram, rhs)
    below = done[:, rhs : 2 * rhs]
    r_ref[...] = done[:, 0:rhs]
    eye = (
        lax.broadcasted_iota(I32, (basis, basis), 0) == lax.broadcasted_iota(I32, (basis, basis), 1)
    ).astype(F32)
    h_ref[...] = dot(eye, h, NT)
    mix = jnp.concatenate([-dot(below, h, NN), below], axis=1)
    mix_high, mix_low = split(mix)

    def finish(q, w, p):
        high, low = split(jnp.concatenate([q[p], w[rhs * p : rhs * (p + 1)]], axis=0))
        out = lax.dot_general(mix_high, high, NN, preferred_element_type=F32)
        out += lax.dot_general(mix_high, low, NN, preferred_element_type=F32)
        out += lax.dot_general(mix_low, high, NN, preferred_element_type=F32)
        return out

    wait_all(copies)
    copies = []
    for s, (q, w, o, hbm) in enumerate(((q_ref, wf_ref, of_ref, nf_hbm), (b_ref, wb_ref, ob_ref, nb_hbm))):
        for p in range(2):
            o[p] = finish(q, w, p)
            copies += start_all([pltpu.make_async_copy(o.at[p], hbm.at[:, p, :], sem.at[s, p])])
    wait_all(copies)


def shape(*dims, dtype=F32):
    return jax.ShapeDtypeStruct(dims, dtype)


def neighbours(axis, step):
    n = lax.axis_size(axis)
    return [(i, i + step) for i in range(n) if 0 <= i + step < n]


def spread(x, axes):
    n = lax.axis_size(axes)
    return lax.all_to_all(jnp.broadcast_to(x[None], (n,) + x.shape), axes, 0, 0, tiled=True)


def body(fem_basis, bem_basis, fem_diagonal, fem_values, fem_columns, halo_rows, bem_matrix, trace_rows, bem_slot):
    blocks, rhs, _, nf = fem_basis.shape
    nb = bem_basis.shape[3]
    nz = fem_values.shape[0]
    width = halo_rows.shape[1]
    slots = trace_rows.shape[0]
    n_row, n_col = lax.axis_size("row"), lax.axis_size("col")
    devices = n_row * n_col
    both = ("row", "col")
    groups = 2 * rhs // SUB
    room = slots // devices
    fold = LANES // room
    if LANES % room or groups % fold:
        fold = 0
    mail_shape = (devices, 4 * rhs // fold, LANES) if fold else (4 * rhs, slots)
    traces = trace_rows.reshape(slots // LANES, LANES)
    owned = bem_slot.reshape(nb // LANES, LANES)
    diagonal = fem_diagonal.reshape(1, nf)
    sizes = (blocks, rhs, nf, nb, width, slots, fold)

    vmem = pl.BlockSpec(memory_space=pltpu.VMEM)
    u, out, mail, phi = pl.pallas_call(
        functools.partial(send_kernel, sizes),
        in_specs=[ANY, ANY, vmem, vmem, vmem],
        out_specs=[vmem] * 4,
        out_shape=[shape(2 * rhs, nf), shape(4, 2 * rhs, width), shape(*mail_shape), shape(2 * rhs, nb, dtype=BF16)],
        scratch_shapes=[pltpu.VMEM((2 * rhs, nb), F32), pltpu.VMEM((nb, LANES), I32), pltpu.SemaphoreType.DMA((4,))],
        name="send",
    )(fem_basis, bem_basis, halo_rows, traces, owned)

    phi_all = spread(phi, "row")
    halos = [
        lax.ppermute(out[0], "col", neighbours("col", 1)),
        lax.ppermute(out[1], "col", neighbours("col", -1)),
        lax.ppermute(out[2], "row", neighbours("row", 1)),
        lax.ppermute(out[3], "row", neighbours("row", -1)),
    ]
    if fold:
        mail = lax.all_to_all(mail, both, 0, 0, tiled=True)
    else:
        mail = lax.all_to_all(mail, both, 1, 1, tiled=True)

    fem_sizes = (rhs, nf, width, nz)
    tiles = nf // LANES
    early = tiles // 2
    own = pl.pallas_call(
        functools.partial(own_kernel, fem_sizes, early),
        in_specs=[vmem] * 4,
        out_specs=vmem,
        out_shape=shape(2 * rhs, nf),
        name="own",
    )(u, fem_columns, fem_values, diagonal)

    k_len = bem_matrix.shape[2]
    full = lambda *dims: pl.BlockSpec(dims, lambda i: (0,) * len(dims))
    partial, fem_part = pl.pallas_call(
        functools.partial(bem_kernel, fem_sizes, early, tiles // n_col),
        grid=(n_col,),
        in_specs=[
            full(n_row, 2 * rhs, nb),
            pl.BlockSpec((2, nb, k_len), lambda i: (0, i, 0)),
            full(2 * rhs, nf),
        ]
        + [full(2 * rhs, width)] * 4
        + [full(nz, nf), full(nz, nf), full(1, nf), full(2 * rhs, nf)],
        out_specs=[pl.BlockSpec((1, 2 * rhs, nb), lambda i: (i, 0, 0)), full(2 * rhs, nf)],
        out_shape=[shape(n_col, 2 * rhs, nb), shape(2 * rhs, nf)],
        name="bem",
    )(phi_all, bem_matrix, u, *halos, fem_columns, fem_values, diagonal, own)

    parts = lax.all_to_all(partial, "col", 0, 0, tiled=True)

    basis = blocks * rhs
    w_fem, add, z_fem = pl.pallas_call(
        functools.partial(trace_kernel, sizes),
        in_specs=[ANY] + [vmem] * 4,
        out_specs=[vmem] * 3,
        out_shape=[shape(2 * rhs, nf), shape(2 * rhs, nb), shape(basis + rhs, LANES)],
        scratch_shapes=[
            pltpu.VMEM((slots, LANES), I32),
            pltpu.VMEM((4 * rhs, slots), F32),
            pltpu.VMEM((2, basis, nf), F32),
            pltpu.SemaphoreType.DMA((2 * blocks,)),
        ],
        name="trace",
    )(fem_basis, fem_part, mail, traces, owned)

    w_bem, local = pl.pallas_call(
        functools.partial(sums_kernel, (blocks, rhs)),
        in_specs=[ANY] + [vmem] * 3,
        out_specs=[vmem] * 2,
        out_shape=[shape(2 * rhs, nb), shape(rhs, LANES)],
        scratch_shapes=[pltpu.VMEM((2, basis, nb), F32), pltpu.SemaphoreType.DMA((2 * blocks,))],
        name="sums",
    )(bem_basis, parts, add, z_fem)

    everyone = spread(local, both)

    next_fem, next_bem, h, r_factor = pl.pallas_call(
        functools.partial(last_kernel, (blocks, rhs, 2.0 * devices * (nf + nb))),
        in_specs=[ANY, ANY] + [vmem] * 3,
        out_specs=[ANY, ANY, vmem, vmem],
        out_shape=[shape(rhs, 2, nf), shape(rhs, 2, nb), shape(basis, rhs), shape(rhs, rhs)],
        scratch_shapes=[
            pltpu.VMEM((2, basis, nf), F32),
            pltpu.VMEM((2, basis, nb), F32),
            pltpu.VMEM((2, rhs, nf), F32),
            pltpu.VMEM((2, rhs, nb), F32),
            pltpu.SemaphoreType.DMA((2, 2 * blocks)),
        ],
        name="last",
    )(fem_basis, bem_basis, everyone, w_fem, w_bem)
    return (next_fem, next_bem, h.reshape(blocks, rhs, rhs), r_factor)


def solution(mesh):
    return jax.shard_map(
        body,
        mesh=mesh,
        in_specs=(
            P(None, None, None, ("row", "col")),
            P(None, None, None, ("row", "col")),
            P(("row", "col")),
            P(None, ("row", "col")),
            P(None, ("row", "col")),
            P(None, ("row", "col")),
            P(None, "row", "col"),
            P(("row", "col")),
            P(("row", "col")),
        ),
        out_specs=(P(None, None, ("row", "col")), P(None, None, ("row", "col")), P(), P()),
        check_vma=False,
    )
```
